32 devices in a mesh: row: 4 (over z), col: 8 (over y, x, core).
Axes of the slice: x: 2, y: 2, z: 4, core: 2. Of those that a mesh axis runs over, the one named last changes fastest.
Arguments:
- trailing: float32 [20480, 20480], P('row', 'col'), may hold values from -24 to 24
- panel_block: float32 [20480, 128], P(('row', 'col')), may hold values from -0.2795085 to 0.2795085
Outputs:
- trailing_out: float32 [20480, 20480], P('row', 'col')
- r_factor: float32 [128, 128], replicated
- first_factor: float32 [128, 128], replicated
The draws below stay inside these ranges and needn't reach their ends.
All inputs are finite; a program needn't handle non-finite values.
Results may differ from the reference program's by a relative error of at most 0.0003.
Values sent between devices are 32-bit elements; how exact they have to be, the bound alone decides.
No kernel may reach another device: no remote copies, remote signals or barrier semaphores. Data moves between devices by JAX's collectives and lax.ppermute only.
A program may use at most 192 MiB of HBM per device.

```python
import math
import jax
import jax.numpy as jnp
from jax import lax

M = 20480
NB = 128


def draw_trailing(key, part):
    noise = jnp.clip(jax.random.normal(key, (M, M), jnp.float32), -6.0, 6.0)
    symmetric = 0.5 * (noise + noise.T)
    return jnp.clip(symmetric, -24.0, 24.0)


def draw_panel_block(key, part):
    spreads = jnp.exp(jax.random.uniform(jax.random.fold_in(key, 3), (NB,), jnp.float32, math.log(0.03), math.log(0.3)))
    rising = 1.0 + 4.0 * jnp.arange(M, dtype=jnp.float32) / (M - 1.0)
    shared = jnp.clip(jax.random.normal(jax.random.fold_in(key, 5), (M,), jnp.float32), -4.0, 4.0)
    private = jnp.clip(jax.random.normal(key, (M, NB), jnp.float32), -4.0, 4.0)
    row_scales = rising
    values = (shared[:, None] + spreads[None, :] * private) * row_scales[:, None] * M ** (-0.5)
    bound = 40.0 * M ** (-0.5)
    return jnp.clip(values, -bound, bound)


def setup_inputs(seed: int = 0) -> dict:
    streams_of = jax.random.split(jax.random.key(seed), 3)
    trailing = draw_trailing(jax.random.fold_in(streams_of[2], 71), 0)
    panel_block = draw_panel_block(jax.random.fold_in(streams_of[2], 71), 0)
    return {"trailing": trailing, "panel_block": panel_block}


HIGHEST = lax.Precision.HIGHEST

def gram_of(block):
    return jnp.dot(block.T.astype(jnp.float32), block.astype(jnp.float32), preferred_element_type=jnp.float32, precision=HIGHEST)

def reference(trailing, panel_block):
    low_one = jnp.linalg.cholesky(gram_of(panel_block))
    first_q = lax.linalg.triangular_solve(low_one, panel_block, left_side=False, lower=True, transpose_a=True)
    low_two = jnp.linalg.cholesky(gram_of(first_q))
    ortho_basis = lax.linalg.triangular_solve(low_two, first_q, left_side=False, lower=True, transpose_a=True)
    r_factor = jnp.dot(low_two.T.astype(jnp.float32), low_one.T.astype(jnp.float32), preferred_element_type=jnp.float32, precision=HIGHEST)
    products = jnp.dot(trailing.astype(jnp.float32), ortho_basis.astype(jnp.float32), preferred_element_type=jnp.float32, precision=HIGHEST)
    projected = jnp.dot(ortho_basis.T.astype(jnp.float32), products.astype(jnp.float32), preferred_element_type=jnp.float32, precision=HIGHEST)
    correction = 2.0 * (products - jnp.dot(ortho_basis.astype(jnp.float32), projected.astype(jnp.float32), preferred_element_type=jnp.float32, precision=HIGHEST))
    left_factor = jnp.concatenate([ortho_basis, correction], axis=1)
    right_factor = jnp.concatenate([correction, ortho_basis], axis=1)
    trailing_out = trailing - jnp.dot(left_factor.astype(jnp.float32), right_factor.T.astype(jnp.float32), preferred_element_type=jnp.float32, precision=HIGHEST)
    return (trailing_out, r_factor, low_one.T)
```

```python
import jax
import jax.numpy as jnp
from jax import lax
from jax.experimental import pallas as pl
from jax.experimental.pallas import tpu as pltpu
from jax.sharding import PartitionSpec as P

HIGHEST = lax.Precision.HIGHEST
F32 = jnp.float32
BF16 = jnp.bfloat16
CHUNKS = 2


def matmul(first, second):
    return jnp.dot(first, second, preferred_element_type=F32, precision=HIGHEST)


def split(block):
    high = block.astype(BF16)
    return high, (block - high.astype(F32)).astype(BF16)


def contract(first, second, dims):
    return lax.dot_general(first, second, (dims, ((), ())), preferred_element_type=F32)


def factor_kernel(gram_ref, upper_ref, inverse_ref):
    order = gram_ref.shape[0]
    step = 8
    lane = lax.broadcasted_iota(jnp.int32, (1, order), 1)
    left = gram_ref[...]
    row_id = lax.broadcasted_iota(jnp.int32, (order, order), 0)
    right = (row_id == lax.broadcasted_iota(jnp.int32, (order, order), 1)).astype(F32)
    for base in range(0, order, step):
        rows_l = [left[base + i:base + i + 1, :] for i in range(step)]
        rows_r = [right[base + i:base + i + 1, :] for i in range(step)]
        pivots = [
            [jnp.broadcast_to(rows_l[i][:, base + j:base + j + 1], (1, order)) for j in range(step)]
            for i in range(step)
        ]
        columns = [
            jnp.broadcast_to(left[:, base + j:base + j + 1], (order, order)) for j in range(step)
        ]
        for j in range(step):
            pivot = pivots[j][j]
            root = lax.rsqrt(pivot)
            root = root * (1.5 - 0.5 * pivot * root * root)
            recip = root * root
            upper_ref[base + j:base + j + 1, :] = jnp.where(lane >= base + j, rows_l[j] * root, 0.0)
            inverse_ref[base + j:base + j + 1, :] = rows_r[j] * root
            for i in range(j + 1, step):
                ratio = pivots[j][i] * recip
                rows_l[i] = rows_l[i] - ratio * rows_l[j]
                rows_r[i] = rows_r[i] - ratio * rows_r[j]
                for k in range(i, step):
                    pivots[i][k] = pivots[i][k] - ratio * pivots[j][k]
                columns[i] = columns[i] - columns[j] * ratio
            if base + step < order:
                scaled = columns[j] * recip
                left = left - scaled * rows_l[j]
                right = right - scaled * rows_r[j]


def factor(gram):
    return pl.pallas_call(
        factor_kernel,
        out_shape=[jax.ShapeDtypeStruct(gram.shape, F32)] * 2,
        name="factor",
    )(gram)


def product_kernel(trailing_ref, basis_ref, out_ref, split_ref):
    width = basis_ref.shape[1]

    @pl.when(pl.program_id(0) == 0)
    def _():
        high, low = split(basis_ref[...])
        split_ref[:, :width] = high
        split_ref[:, width:] = low

    high, low = split(trailing_ref[...])
    both = contract(high, split_ref[...], ((1,), (0,)))
    small = contract(low, split_ref[:, :width], ((1,), (0,)))
    out_ref[0] = both[:, :width] + both[:, width:] + small


def product(trailing, basis, pieces, chunk):
    height, depth = trailing.shape
    width = basis.shape[1]
    rows = height // pieces // CHUNKS
    return pl.pallas_call(
        product_kernel,
        grid=(pieces,),
        in_specs=[
            pl.BlockSpec((rows, depth), lambda i: (i * CHUNKS + chunk, 0)),
            pl.BlockSpec((depth, width), lambda i: (0, 0)),
        ],
        out_specs=pl.BlockSpec((1, rows, width), lambda i: (i, 0, 0)),
        out_shape=jax.ShapeDtypeStruct((pieces, rows, width), F32),
        scratch_shapes=[pltpu.VMEM((depth, 2 * width), BF16)],
        name="product",
    )(trailing, basis)


def update_kernel(trailing_ref, left_a_ref, left_b_ref, right_ref, out_ref, high_ref, low_ref):
    @pl.when(pl.program_id(0) == 0)
    def _():
        high_ref[...], low_ref[...] = split(right_ref[...])

    left = jnp.concatenate([left_a_ref[...], left_b_ref[...]], axis=1)
    high, low = split(left)
    dims = ((1,), (1,))
    change = contract(high, high_ref[...], dims)
    change = change + contract(high, low_ref[...], dims)
    change = change + contract(low, high_ref[...], dims)
    out_ref[...] = trailing_ref[...] - change


def update(trailing, left_a, left_b, right):
    height, depth = trailing.shape
    width = left_a.shape[1]
    rows = 256
    return pl.pallas_call(
        update_kernel,
        grid=(height // rows,),
        in_specs=[
            pl.BlockSpec((rows, depth), lambda i: (i, 0)),
            pl.BlockSpec((rows, width), lambda i: (i, 0)),
            pl.BlockSpec((rows, width), lambda i: (i, 0)),
            pl.BlockSpec((depth, 2 * width), lambda i: (0, 0)),
        ],
        out_specs=pl.BlockSpec((rows, depth), lambda i: (i, 0)),
        out_shape=jax.ShapeDtypeStruct((height, depth), F32),
        scratch_shapes=[pltpu.VMEM((depth, 2 * width), BF16)] * 2,
        name="update",
    )(trailing, left_a, left_b, right)


def bits_of(size):
    return size.bit_length() - 1


def swap(block, axis, mask):
    size = lax.axis_size(axis)
    return lax.ppermute(block, axis, [(i, i ^ mask) for i in range(size)])


def sum_over(block, axis):
    bits = list(range(bits_of(lax.axis_size(axis))))
    groups = []
    if len(bits) % 2:
        groups.append(bits[:1])
        bits = bits[1:]
    while bits:
        groups.append(bits[:2])
        bits = bits[2:]
    for group in groups:
        if len(group) == 1:
            block = block + swap(block, axis, 1 << group[0])
        else:
            low, high = 1 << group[0], 1 << group[1]
            one = swap(block, axis, low)
            two = swap(block, axis, high)
            three = swap(block, axis, low | high)
            block = (block + one) + (two + three)
    return block


def reversed_axes(block, count):
    order = tuple(reversed(range(count))) + tuple(range(count, block.ndim))
    return jnp.transpose(block, order)


def stage_swap(block, axis, low_bit, high_bit):
    size = lax.axis_size(axis)
    perm = [(i, i ^ (1 << (high_bit if i & 1 else low_bit))) for i in range(size)]
    return lax.ppermute(block, axis, perm)


def stage_bit(index, low_bit, high_bit):
    return jnp.where(index & 1 == 0, (index >> low_bit) & 1, (index >> high_bit) & 1)


def gather_over(block, axis):
    size = lax.axis_size(axis)
    count = bits_of(size)
    index = lax.axis_index(axis)
    odd = index & 1
    for stage in range(count - 1):
        low_bit, high_bit = stage + 1, count - 1 - stage
        other = stage_swap(block, axis, low_bit, high_bit)
        mine = stage_bit(index, low_bit, high_bit)
        block = jnp.where(mine == 0, jnp.stack([block, other]), jnp.stack([other, block]))
    if count > 2:
        block = jnp.where(odd == 0, block, reversed_axes(block, count - 1))
    other = swap(block, axis, 1)
    where = count - 1
    block = jnp.where(
        odd == 0, jnp.stack([block, other], axis=where), jnp.stack([other, block], axis=where)
    )
    return block.reshape((size,) + block.shape[count:])


def scatter_sum_over(block, axis):
    size = lax.axis_size(axis)
    count = bits_of(size)
    index = lax.axis_index(axis)
    odd = index & 1
    block = block.reshape((size // 2, 2) + block.shape[1:])
    even_half, odd_half = block[:, 0], block[:, 1]
    sent = jnp.where(odd == 0, odd_half, even_half)
    kept = jnp.where(odd == 0, even_half, odd_half)
    block = kept + swap(sent, axis, 1)
    block = block.reshape((2,) * (count - 1) + block.shape[1:])
    if count > 2:
        block = jnp.where(odd == 0, block, reversed_axes(block, count - 1))
    for stage in range(count - 1):
        low_bit, high_bit = count - 1 - stage, stage + 1
        mine = stage_bit(index, low_bit, high_bit)
        sent = jnp.where(mine == 0, block[1], block[0])
        kept = jnp.where(mine == 0, block[0], block[1])
        block = kept + stage_swap(sent, axis, low_bit, high_bit)
    return block


def column_pieces(block, row, column):
    row_devices = lax.axis_size("row")
    col_devices = lax.axis_size("col")
    per_owner = col_devices // row_devices
    received = []
    for turn in range(row_devices):
        perm = []
        for r in range(row_devices):
            for c in range(col_devices):
                target_row = r ^ (c % row_devices) ^ turn
                target_col = per_owner * r + c // row_devices
                perm.append((r * col_devices + c, target_row * col_devices + target_col))
        received.append(lax.ppermute(block, ("row", "col"), perm))
    count = bits_of(row_devices)
    pieces = jnp.stack(received).reshape((2,) * count + block.shape)
    mask = row ^ (column // per_owner)
    for bit in range(count):
        axis = count - 1 - bit
        pieces = jnp.where((mask >> bit) & 1 == 0, pieces, jnp.flip(pieces, axis))
    return pieces.reshape((row_devices,) + block.shape)


def on_device(trailing, panel_block):
    col_devices = lax.axis_size("col")
    row = lax.axis_index("row")
    column = lax.axis_index("col")
    height, depth = trailing.shape
    rows, width = panel_block.shape
    part = rows // CHUNKS

    gram_one = sum_over(sum_over(matmul(panel_block.T, panel_block), "col"), "row")
    upper_one, inverse_one = factor(gram_one)
    panel_rows = gather_over(panel_block, "col").reshape(height, width)
    panel_cols = column_pieces(panel_block, row, column).reshape(depth, width)
    first_rows = matmul(panel_rows, inverse_one.T)
    first_cols = matmul(panel_cols, inverse_one.T)
    gram_two = sum_over(matmul(first_rows.T, first_rows), "row")
    upper_two, inverse_two = factor(gram_two)
    r_factor = matmul(upper_two, upper_one)

    first_pieces = first_rows.reshape(col_devices, CHUNKS, part, width)
    inner = jnp.zeros((width, width), F32)
    whole_rows, whole_cols = [], []
    for chunk in range(CHUNKS):
        partial = product(trailing, first_cols, col_devices, chunk)
        inner = inner + lax.dot_general(
            first_pieces[:, chunk],
            partial,
            (((0, 1), (0, 1)), ((), ())),
            precision=HIGHEST,
            preferred_element_type=F32,
        )
        mine = scatter_sum_over(partial, "col")
        whole_rows.append(gather_over(mine, "col"))
        whole_cols.append(column_pieces(mine, row, column))
    inner = sum_over(sum_over(inner, "col"), "row")
    product_rows = jnp.stack(whole_rows, axis=1).reshape(height, width)
    product_cols = jnp.stack(whole_cols, axis=1).reshape(depth, width)

    metric = matmul(inverse_two.T, inverse_two)
    middle = matmul(matmul(metric, inner), metric)
    middle = middle + middle.T
    right = 2.0 * jnp.concatenate(
        [
            matmul(product_cols, metric) - matmul(first_cols, middle),
            matmul(first_cols, metric),
        ],
        axis=1,
    )
    trailing_out = update(trailing, first_rows, product_rows, right)
    return (trailing_out, r_factor, upper_one)


def solution(mesh):
    in_specs = (P("row", "col"), P(("row", "col"), None))
    out_specs = (P("row", "col"), P(), P())
    return jax.shard_map(
        on_device, mesh=mesh, in_specs=in_specs, out_specs=out_specs, check_vma=False
    )
```

```python
import functools

import jax
import jax.numpy as jnp
from jax import lax
from jax.experimental import pallas as pl
from jax.experimental.pallas import tpu as pltpu
from jax.sharding import PartitionSpec as P


HIGHEST = lax.Precision.HIGHEST
F32 = jnp.float32
BF16 = jnp.bfloat16
PRODUCT_GROUPS = ((0, 1, 2), (3,))
UPDATE_GROUPS = ((0, 1), (2, 3))
BUFFERS = 4
VMEM_LIMIT = 60 * 1024 * 1024


def matmul(first, second):
    return jnp.dot(first, second, preferred_element_type=F32, precision=HIGHEST)


def split(block):
    high = block.astype(BF16)
    return high, (block - high.astype(F32)).astype(BF16)


def contract(first, second, dims):
    return lax.dot_general(first, second, (dims, ((), ())), preferred_element_type=F32)


def factor_kernel(gram_ref, upper_ref, inverse_ref):
    order = gram_ref.shape[0]
    step = 8
    lane = lax.broadcasted_iota(jnp.int32, (1, order), 1)
    left = gram_ref[...]
    row_id = lax.broadcasted_iota(jnp.int32, (order, order), 0)
    right = (row_id == lax.broadcasted_iota(jnp.int32, (order, order), 1)).astype(F32)
    for base in range(0, order, step):
        rows_l = [left[base + i:base + i + 1, :] for i in range(step)]
        rows_r = [right[base + i:base + i + 1, :] for i in range(step)]
        pivots = [
            [jnp.broadcast_to(rows_l[i][:, base + j:base + j + 1], (1, order)) for j in range(step)]
            for i in range(step)
        ]
        columns = [
            jnp.broadcast_to(left[:, base + j:base + j + 1], (order, order)) for j in range(step)
        ]
        for j in range(step):
            pivot = pivots[j][j]
            root = lax.rsqrt(pivot)
            root = root * (1.5 - 0.5 * pivot * root * root)
            recip = root * root
            upper_ref[base + j:base + j + 1, :] = jnp.where(lane >= base + j, rows_l[j] * root, 0.0)
            inverse_ref[base + j:base + j + 1, :] = rows_r[j] * root
            for i in range(j + 1, step):
                ratio = pivots[j][i] * recip
                rows_l[i] = rows_l[i] - ratio * rows_l[j]
                rows_r[i] = rows_r[i] - ratio * rows_r[j]
                for k in range(i, step):
                    pivots[i][k] = pivots[i][k] - ratio * pivots[j][k]
                columns[i] = columns[i] - columns[j] * ratio
            if base + step < order:
                scaled = columns[j] * recip
                left = left - scaled * rows_l[j]
                right = right - scaled * rows_r[j]


def factor(gram):
    return pl.pallas_call(
        factor_kernel,
        out_shape=[jax.ShapeDtypeStruct(gram.shape, F32)] * 2,
        name="factor",
    )(gram)


def contract_split(first, second, dims):
    out = contract(first[0], second[0], dims)
    out = out + contract(first[0], second[1], dims)
    return out + contract(first[1], second[0], dims)


def blocking(rows, count):
    sub = 2 if rows % 16 == 0 and count > 1 else 1
    return sub, rows // sub


def product_kernel(count, has_start, *refs):
    (cols_ref, order_ref, trailing_ref), refs = refs[:3], refs[3:]
    basis_refs, refs = refs[:count], refs[count:]
    if has_start:
        start_ref, refs = refs[0], refs[1:]
    out_ref, split_ref, buffer_ref, before_ref, result_ref, in_sems, out_sems = refs
    buffers, block, _ = buffer_ref.shape
    piece, width = basis_refs[0].shape
    height = out_ref.shape[0]
    pieces = order_ref.shape[0]
    rows = height // pieces
    sub = rows // block
    steps = height // block

    def window(step):
        return pl.ds(pl.multiple_of(step * block, 8), block)

    def in_copies(step):
        slot = lax.rem(step, buffers)
        top = order_ref[step // sub] * rows + lax.rem(step, sub) * block
        top = pl.multiple_of(top, 8)
        out = []
        for i in range(count):
            left = cols_ref[i] * piece
            if piece % 128 == 0:
                left = pl.multiple_of(left, 128)
            source = trailing_ref.at[pl.ds(top, block), pl.ds(left, piece)]
            target = buffer_ref.at[slot, :, pl.ds(i * piece, piece)]
            out.append(pltpu.make_async_copy(source, target, in_sems.at[slot, i]))
        if has_start:
            source = start_ref.at[window(step), :]
            out.append(pltpu.make_async_copy(source, before_ref.at[slot], in_sems.at[slot, count]))
        return out

    def out_copy(step):
        slot = lax.rem(step, buffers)
        return pltpu.make_async_copy(result_ref.at[slot], out_ref.at[window(step), :], out_sems.at[slot])

    for step in range(min(buffers - 1, steps)):
        for copy in in_copies(jnp.int32(step)):
            copy.start()
    for i, basis_ref in enumerate(basis_refs):
        high, low = split(basis_ref[...])
        split_ref[i * piece:(i + 1) * piece, :width] = high
        split_ref[i * piece:(i + 1) * piece, width:] = low

    def body(step, carry):
        @pl.when(step + buffers - 1 < steps)
        def _():
            for copy in in_copies(step + buffers - 1):
                copy.start()

        for copy in in_copies(step):
            copy.wait()

        @pl.when(step >= buffers)
        def _():
            out_copy(step - buffers).wait()

        slot = lax.rem(step, buffers)
        high, low = split(buffer_ref[slot])
        both = contract(high, split_ref[...], ((1,), (0,)))
        small = contract(low, split_ref[:, :width], ((1,), (0,)))
        total = both[:, :width] + both[:, width:] + small
        if has_start:
            total = total + before_ref[slot]
        result_ref[slot] = total
        out_copy(step).start()
        return carry

    lax.fori_loop(0, steps, body, 0)
    for step in range(max(steps - buffers, 0), steps):
        out_copy(jnp.int32(step)).wait()


def product(trailing, basis, columns, order, start):
    height = trailing.shape[0]
    count = len(basis)
    piece, width = basis[0].shape
    _, block = blocking(height // order.shape[0], count)
    args = [columns, order, trailing, *basis]
    smem = pl.BlockSpec(memory_space=pltpu.SMEM)
    vmem = pl.BlockSpec(memory_space=pltpu.VMEM)
    hbm = pl.BlockSpec(memory_space=pl.ANY)
    in_specs = [smem, smem, hbm] + [vmem] * count
    if start is not None:
        args.append(start)
        in_specs.append(hbm)
    return pl.pallas_call(
        functools.partial(product_kernel, count, start is not None),
        in_specs=in_specs,
        out_specs=hbm,
        out_shape=jax.ShapeDtypeStruct((height, width), F32),
        scratch_shapes=[
            pltpu.VMEM((count * piece, 2 * width), BF16),
            pltpu.VMEM((BUFFERS, block, count * piece), F32),
            pltpu.VMEM((BUFFERS, block, width), F32),
            pltpu.VMEM((BUFFERS, block, width), F32),
            pltpu.SemaphoreType.DMA((BUFFERS, count + 1)),
            pltpu.SemaphoreType.DMA((BUFFERS,)),
        ],
        compiler_params=pltpu.CompilerParams(vmem_limit_bytes=VMEM_LIMIT),
        name="product",
    )(*args)


def update_kernel(count, has_start, *refs):
    (cols_ref, order_ref, trailing_ref, left_a_ref, left_b_ref), refs = refs[:5], refs[5:]
    right_a_refs, refs = refs[:count], refs[count:]
    right_b_refs, refs = refs[:count], refs[count:]
    (metric_ref, middle_ref), refs = refs[:2], refs[2:]
    if has_start:
        refs = refs[1:]
    out_ref, split_ref, in_ref, la_ref, lb_ref, result_ref, in_sems, out_sems = refs
    buffers, block, _ = in_ref.shape
    piece, width = right_a_refs[0].shape
    height = trailing_ref.shape[0]
    pieces = order_ref.shape[0]
    rows = height // pieces
    sub = rows // block
    steps = height // block

    def window(ref, step, i):
        top = order_ref[step // sub] * rows + lax.rem(step, sub) * block
        left = cols_ref[i] * piece
        if piece % 128 == 0:
            left = pl.multiple_of(left, 128)
        return ref.at[pl.ds(pl.multiple_of(top, 8), block), pl.ds(left, piece)]

    def in_copies(step):
        slot = lax.rem(step, buffers)
        out = []
        for i in range(count):
            target = in_ref.at[slot, :, pl.ds(i * piece, piece)]
            out.append(pltpu.make_async_copy(window(trailing_ref, step, i), target, in_sems.at[slot, i]))
        where = pl.ds(pl.multiple_of(step * block, 8), block)
        out.append(pltpu.make_async_copy(left_a_ref.at[where, :], la_ref.at[slot], in_sems.at[slot, count]))
        out.append(pltpu.make_async_copy(left_b_ref.at[where, :], lb_ref.at[slot], in_sems.at[slot, count + 1]))
        return out

    def out_copies(step):
        slot = lax.rem(step, buffers)
        out = []
        for i in range(count):
            source = result_ref.at[slot, :, pl.ds(i * piece, piece)]
            out.append(pltpu.make_async_copy(source, window(out_ref, step, i), out_sems.at[slot, i]))
        return out

    for step in range(buffers - 1):
        for copy in in_copies(jnp.int32(step)):
            copy.start()
    dims = ((1,), (0,))
    metric = split(metric_ref[...])
    middle = split(middle_ref[...])
    for i in range(count):
        basis = split(right_a_refs[i][...])
        prods = split(right_b_refs[i][...])
        first = contract_split(prods, metric, dims) - contract_split(basis, middle, dims)
        second = contract_split(basis, metric, dims)
        high, low = split(jnp.concatenate([first + first, second + second], axis=1))
        where = pl.ds(i * piece, piece)
        split_ref[where, : 2 * width] = high
        split_ref[where, 2 * width : 4 * width] = low
        split_ref[where, 4 * width :] = high

    def body(step, carry):
        @pl.when(step + buffers - 1 < steps)
        def _():
            for copy in in_copies(step + buffers - 1):
                copy.start()

        for copy in in_copies(step):
            copy.wait()

        @pl.when(step >= buffers)
        def _():
            for copy in out_copies(step - buffers):
                copy.wait()

        slot = lax.rem(step, buffers)
        high, low = split(jnp.concatenate([la_ref[slot], lb_ref[slot]], axis=1))
        left = jnp.concatenate([high, high, low], axis=1)
        change = contract(left, split_ref[...], ((1,), (1,)))
        result_ref[slot] = in_ref[slot] - change
        for copy in out_copies(step):
            copy.start()
        return carry

    lax.fori_loop(0, steps, body, 0)
    for step in range(max(steps - buffers, 0), steps):
        for copy in out_copies(jnp.int32(step)):
            copy.wait()


def update(trailing, left_a, left_b, right_a, right_b, metric, middle, columns, order, start):
    height, depth = trailing.shape
    count = len(right_a)
    piece, width = right_a[0].shape
    _, block = blocking(height // order.shape[0], count)
    smem = pl.BlockSpec(memory_space=pltpu.SMEM)
    vmem = pl.BlockSpec(memory_space=pltpu.VMEM)
    hbm = pl.BlockSpec(memory_space=pl.ANY)
    args = [columns, order, trailing, left_a, left_b, *right_a, *right_b, metric, middle]
    in_specs = [smem, smem, hbm, hbm, hbm] + [vmem] * (2 * count + 2)
    aliases = {}
    if start is not None:
        aliases = {len(args): 0}
        args.append(start)
        in_specs.append(hbm)
    return pl.pallas_call(
        functools.partial(update_kernel, count, start is not None),
        in_specs=in_specs,
        out_specs=hbm,
        out_shape=jax.ShapeDtypeStruct((height, depth), F32),
        input_output_aliases=aliases,
        scratch_shapes=[
            pltpu.VMEM((count * piece, 6 * width), BF16),
            pltpu.VMEM((BUFFERS, block, count * piece), F32),
            pltpu.VMEM((BUFFERS, block, width), F32),
            pltpu.VMEM((BUFFERS, block, width), F32),
            pltpu.VMEM((BUFFERS, block, count * piece), F32),
            pltpu.SemaphoreType.DMA((BUFFERS, count + 2)),
            pltpu.SemaphoreType.DMA((BUFFERS, count)),
        ],
        compiler_params=pltpu.CompilerParams(vmem_limit_bytes=VMEM_LIMIT),
        name="update",
    )(*args)


def bits_of(size):
    return size.bit_length() - 1


def swap(block, axis, mask):
    size = lax.axis_size(axis)
    return lax.ppermute(block, axis, [(i, i ^ mask) for i in range(size)])


def sum_over_all(block):
    for axis in ("row", "col"):
        for bit in range(bits_of(lax.axis_size(axis))):
            other = swap(block, axis, 1 << bit)
            block = block + other
    return block


def stage_masks(count, stage):
    if stage == count - 1:
        return 1, 1
    return 1 << (stage + 1), 1 << (count - 1 - stage)


def stage_swap(block, axis, stage):
    size = lax.axis_size(axis)
    masks = stage_masks(bits_of(size), stage)
    return lax.ppermute(block, axis, [(i, i ^ masks[i & 1]) for i in range(size)])


def gather_masks(count, odd, stages):
    if stages == 0:
        return [0]
    mask = stage_masks(count, stages - 1)[odd]
    own = gather_masks(count, odd, stages - 1)
    other = gather_masks(count, odd ^ (mask & 1), stages - 1)
    return own + [mask ^ m for m in other]


def gather_over(block, axis):
    for stage in range(bits_of(lax.axis_size(axis))):
        other = stage_swap(block, axis, stage)
        block = jnp.concatenate([block, other])
    return block


def scatter_sum_over(block, axis):
    for stage in reversed(range(bits_of(lax.axis_size(axis)))):
        half = block.shape[0] // 2
        other = stage_swap(block[half:], axis, stage)
        block = block[:half] + other
    return block


def by_parity(index, even, odd):
    return jnp.where(index & 1 == 0, jnp.array(even, jnp.int32), jnp.array(odd, jnp.int32))


def rotate_right(index, size):
    return (index >> 1) | ((index & 1) * (size >> 1))


def rotate_left(index, size):
    return ((index << 1) & (size - 1)) | (index >> (bits_of(size) - 1))


def column_pieces(block):
    row_devices = lax.axis_size("row")
    col_devices = lax.axis_size("col")
    per_owner = col_devices // row_devices
    received = []
    for turn in range(row_devices):
        perm = []
        for r in range(row_devices):
            for c in range(col_devices):
                target_row = r ^ rotate_right(c % row_devices, row_devices) ^ turn
                target_col = per_owner * r + c // row_devices
                perm.append((r * col_devices + c, target_row * col_devices + target_col))
        received.append(lax.ppermute(block, ("row", "col"), perm))
    return received


def in_index_order(received, mask):
    count = bits_of(len(received))
    shape = received[0].shape
    pieces = jnp.stack(received).reshape((2,) * count + shape)
    for bit in range(count):
        pieces = jnp.where((mask >> bit) & 1 == 0, pieces, jnp.flip(pieces, count - 1 - bit))
    pieces = pieces.reshape((len(received),) + shape)
    order = [rotate_right(i, len(received)) for i in range(len(received))]
    return [jnp.concatenate([pieces[i] for i in order])]


def groups_of(groups, count):
    if count == sum(len(group) for group in groups):
        return groups
    return (tuple(range(count)),)


def on_device(trailing, panel_block):
    row_devices = lax.axis_size("row")
    col_devices = lax.axis_size("col")
    row = lax.axis_index("row")
    column = lax.axis_index("col")
    rows, width = panel_block.shape
    mask = row ^ (column // (col_devices // row_devices))
    count = bits_of(col_devices)
    order = column ^ by_parity(column, *[gather_masks(count, odd, count) for odd in (0, 1)])
    narrow = rows % 128 != 0

    gram_one = sum_over_all(matmul(panel_block.T, panel_block))
    upper_one, inverse_one = factor(gram_one)
    panel_rows = gather_over(panel_block, "col")
    panel_cols = column_pieces(panel_block)
    if narrow:
        panel_cols = in_index_order(panel_cols, mask)
    pieces = len(panel_cols)
    columns = [jnp.zeros((1,), jnp.int32) if narrow else rotate_left(mask ^ i, pieces)[None] for i in range(pieces)]

    def pick(group, blocks):
        return [blocks[i] for i in group], jnp.concatenate([columns[i] for i in group])

    first_cols = [matmul(block, inverse_one.T) for block in panel_cols]
    own = matmul(panel_block, inverse_one.T)
    gram_two = matmul(own.T, own)
    partial = None
    for group in groups_of(PRODUCT_GROUPS, pieces):
        blocks, cols = pick(group, first_cols)
        partial = product(trailing, blocks, cols, order, partial)
    first_rows = matmul(panel_rows, inverse_one.T)
    inner = jnp.dot(first_rows.T, partial, preferred_element_type=F32, precision=lax.Precision.HIGH)
    sums = sum_over_all(jnp.concatenate([inner, gram_two]))
    inner, gram_two = sums[:width], sums[width:]
    mine = scatter_sum_over(partial, "col")
    product_cols = column_pieces(mine)
    if narrow:
        product_cols = in_index_order(product_cols, mask)
    product_rows = gather_over(mine, "col")

    upper_two, inverse_two = factor(gram_two)
    r_factor = matmul(upper_two, upper_one)
    metric = matmul(inverse_two.T, inverse_two)
    middle = matmul(matmul(metric, inner), metric)
    middle = middle + middle.T
    trailing_out = None
    for group in groups_of(UPDATE_GROUPS, pieces):
        right_a, cols = pick(group, first_cols)
        right_b, cols = pick(group, product_cols)
        trailing_out = update(
            trailing, first_rows, product_rows, right_a, right_b, metric, middle, cols, order, trailing_out
        )
    return (trailing_out, r_factor, upper_one)


def solution(mesh):
    in_specs = (P("row", "col"), P(("row", "col"), None))
    out_specs = (P("row", "col"), P(), P())

    return jax.shard_map(
        on_device, mesh=mesh, in_specs=in_specs, out_specs=out_specs, check_vma=False
    )
```

```python
import functools

import jax
import jax.numpy as jnp
from jax import lax
from jax.experimental import pallas as pl
from jax.experimental.pallas import tpu as pltpu
from jax.sharding import PartitionSpec as P


HIGHEST = lax.Precision.HIGHEST
F32 = jnp.float32
BF16 = jnp.bfloat16
PRODUCT_GROUPS = ((0, 1, 2), (3,))
UPDATE_GROUPS = ((0, 1), (2, 3))
BUFFERS = 4
VMEM_LIMIT = 60 * 1024 * 1024


def matmul(first, second):
    return jnp.dot(first, second, preferred_element_type=F32, precision=HIGHEST)


def split(block):
    high = block.astype(BF16)
    return high, (block - high.astype(F32)).astype(BF16)


def contract(first, second, dims):
    return lax.dot_general(first, second, (dims, ((), ())), preferred_element_type=F32)


def factor_kernel(gram_ref, upper_ref, inverse_ref):
    order = gram_ref.shape[0]
    step = 8
    lane = lax.broadcasted_iota(jnp.int32, (1, order), 1)
    left = gram_ref[...]
    row_id = lax.broadcasted_iota(jnp.int32, (order, order), 0)
    right = (row_id == lax.broadcasted_iota(jnp.int32, (order, order), 1)).astype(F32)
    for base in range(0, order, step):
        rows_l = [left[base + i:base + i + 1, :] for i in range(step)]
        rows_r = [right[base + i:base + i + 1, :] for i in range(step)]
        pivots = [
            [jnp.broadcast_to(rows_l[i][:, base + j:base + j + 1], (1, order)) for j in range(step)]
            for i in range(step)
        ]
        columns = [
            jnp.broadcast_to(left[:, base + j:base + j + 1], (order, order)) for j in range(step)
        ]
        for j in range(step):
            pivot = pivots[j][j]
            root = lax.rsqrt(pivot)
            root = root * (1.5 - 0.5 * pivot * root * root)
            recip = root * root
            upper_ref[base + j:base + j + 1, :] = jnp.where(lane >= base + j, rows_l[j] * root, 0.0)
            inverse_ref[base + j:base + j + 1, :] = rows_r[j] * root
            for i in range(j + 1, step):
                ratio = pivots[j][i] * recip
                rows_l[i] = rows_l[i] - ratio * rows_l[j]
                rows_r[i] = rows_r[i] - ratio * rows_r[j]
                for k in range(i, step):
                    pivots[i][k] = pivots[i][k] - ratio * pivots[j][k]
                columns[i] = columns[i] - columns[j] * ratio
            if base + step < order:
                scaled = columns[j] * recip
                left = left - scaled * rows_l[j]
                right = right - scaled * rows_r[j]


def factor(gram):
    return pl.pallas_call(
        factor_kernel,
        out_shape=[jax.ShapeDtypeStruct(gram.shape, F32)] * 2,
        name="factor",
    )(gram)


def contract_split(first, second, dims):
    out = contract(first[0], second[0], dims)
    out = out + contract(first[0], second[1], dims)
    return out + contract(first[1], second[0], dims)


def blocking(rows, count):
    sub = 2 if rows % 16 == 0 and count > 1 else 1
    return sub, rows // sub


def product_kernel(count, has_start, *refs):
    (cols_ref, order_ref, trailing_ref), refs = refs[:3], refs[3:]
    basis_refs, refs = refs[:count], refs[count:]
    if has_start:
        start_ref, refs = refs[0], refs[1:]
    out_ref, split_ref, buffer_ref, before_ref, result_ref, in_sems, out_sems = refs
    buffers, block, _ = buffer_ref.shape
    piece, width = basis_refs[0].shape
    height = out_ref.shape[0]
    pieces = order_ref.shape[0]
    rows = height // pieces
    sub = rows // block
    steps = height // block

    def window(step):
        return pl.ds(pl.multiple_of(step * block, 8), block)

    def in_copies(step):
        slot = lax.rem(step, buffers)
        top = order_ref[step // sub] * rows + lax.rem(step, sub) * block
        top = pl.multiple_of(top, 8)
        out = []
        for i in range(count):
            left = cols_ref[i] * piece
            if piece % 128 == 0:
                left = pl.multiple_of(left, 128)
            source = trailing_ref.at[pl.ds(top, block), pl.ds(left, piece)]
            target = buffer_ref.at[slot, :, pl.ds(i * piece, piece)]
            out.append(pltpu.make_async_copy(source, target, in_sems.at[slot, i]))
        if has_start:
            source = start_ref.at[window(step), :]
            out.append(pltpu.make_async_copy(source, before_ref.at[slot], in_sems.at[slot, count]))
        return out

    def out_copy(step):
        slot = lax.rem(step, buffers)
        return pltpu.make_async_copy(result_ref.at[slot], out_ref.at[window(step), :], out_sems.at[slot])

    for step in range(min(buffers - 1, steps)):
        for copy in in_copies(jnp.int32(step)):
            copy.start()
    for i, basis_ref in enumerate(basis_refs):
        high, low = split(basis_ref[...])
        split_ref[i * piece:(i + 1) * piece, :width] = high
        split_ref[i * piece:(i + 1) * piece, width:] = low

    def body(step, carry):
        @pl.when(step + buffers - 1 < steps)
        def _():
            for copy in in_copies(step + buffers - 1):
                copy.start()

        for copy in in_copies(step):
            copy.wait()

        @pl.when(step >= buffers)
        def _():
            out_copy(step - buffers).wait()

        slot = lax.rem(step, buffers)
        high, low = split(buffer_ref[slot])
        both = contract(high, split_ref[...], ((1,), (0,)))
        small = contract(low, split_ref[:, :width], ((1,), (0,)))
        total = both[:, :width] + both[:, width:] + small
        if has_start:
            total = total + before_ref[slot]
        result_ref[slot] = total
        out_copy(step).start()
        return carry

    lax.fori_loop(0, steps, body, 0)
    for step in range(max(steps - buffers, 0), steps):
        out_copy(jnp.int32(step)).wait()


def product(trailing, basis, columns, order, start):
    height = trailing.shape[0]
    count = len(basis)
    piece, width = basis[0].shape
    _, block = blocking(height // order.shape[0], count)
    args = [columns, order, trailing, *basis]
    smem = pl.BlockSpec(memory_space=pltpu.SMEM)
    vmem = pl.BlockSpec(memory_space=pltpu.VMEM)
    hbm = pl.BlockSpec(memory_space=pl.ANY)
    in_specs = [smem, smem, hbm] + [vmem] * count
    if start is not None:
        args.append(start)
        in_specs.append(hbm)
    return pl.pallas_call(
        functools.partial(product_kernel, count, start is not None),
        in_specs=in_specs,
        out_specs=hbm,
        out_shape=jax.ShapeDtypeStruct((height, width), F32),
        scratch_shapes=[
            pltpu.VMEM((count * piece, 2 * width), BF16),
            pltpu.VMEM((BUFFERS, block, count * piece), F32),
            pltpu.VMEM((BUFFERS, block, width), F32),
            pltpu.VMEM((BUFFERS, block, width), F32),
            pltpu.SemaphoreType.DMA((BUFFERS, count + 1)),
            pltpu.SemaphoreType.DMA((BUFFERS,)),
        ],
        compiler_params=pltpu.CompilerParams(vmem_limit_bytes=VMEM_LIMIT),
        name="product",
    )(*args)


def basis_kernel(count, *refs):
    inverse = refs[0][...]
    for source, target in zip(refs[1:count + 1], refs[count + 1:]):
        target[...] = lax.dot_general(
            source[...], inverse, (((1,), (1,)), ((), ())), precision=HIGHEST, preferred_element_type=F32
        )


def basis_pieces(panel_pieces, inverse):
    count = len(panel_pieces)
    if count == 1:
        return [matmul(panel_pieces[0], inverse.T)]
    return pl.pallas_call(
        functools.partial(basis_kernel, count),
        out_shape=[jax.ShapeDtypeStruct(piece.shape, F32) for piece in panel_pieces],
        name="basis",
    )(inverse, *panel_pieces)


def update_kernel(count, has_start, *refs):
    (cols_ref, order_ref, trailing_ref, left_a_ref, left_b_ref), refs = refs[:5], refs[5:]
    right_a_refs, refs = refs[:count], refs[count:]
    right_b_refs, refs = refs[:count], refs[count:]
    (metric_ref, middle_ref), refs = refs[:2], refs[2:]
    if has_start:
        refs = refs[1:]
    out_ref, split_ref, in_ref, la_ref, lb_ref, result_ref, in_sems, out_sems = refs
    buffers, block, _ = in_ref.shape
    piece, width = right_a_refs[0].shape
    height = trailing_ref.shape[0]
    pieces = order_ref.shape[0]
    rows = height // pieces
    sub = rows // block
    steps = height // block

    def window(ref, step, i):
        top = order_ref[step // sub] * rows + lax.rem(step, sub) * block
        left = cols_ref[i] * piece
        if piece % 128 == 0:
            left = pl.multiple_of(left, 128)
        return ref.at[pl.ds(pl.multiple_of(top, 8), block), pl.ds(left, piece)]

    def in_copies(step):
        slot = lax.rem(step, buffers)
        out = []
        for i in range(count):
            target = in_ref.at[slot, :, pl.ds(i * piece, piece)]
            out.append(pltpu.make_async_copy(window(trailing_ref, step, i), target, in_sems.at[slot, i]))
        where = pl.ds(pl.multiple_of(step * block, 8), block)
        out.append(pltpu.make_async_copy(left_a_ref.at[where, :], la_ref.at[slot], in_sems.at[slot, count]))
        out.append(pltpu.make_async_copy(left_b_ref.at[where, :], lb_ref.at[slot], in_sems.at[slot, count + 1]))
        return out

    def out_copies(step):
        slot = lax.rem(step, buffers)
        out = []
        for i in range(count):
            source = result_ref.at[slot, :, pl.ds(i * piece, piece)]
            out.append(pltpu.make_async_copy(source, window(out_ref, step, i), out_sems.at[slot, i]))
        return out

    for step in range(buffers - 1):
        for copy in in_copies(jnp.int32(step)):
            copy.start()
    dims = ((1,), (0,))
    metric = split(metric_ref[...])
    middle = split(middle_ref[...])
    for i in range(count):
        basis = split(right_a_refs[i][...])
        prods = split(right_b_refs[i][...])
        first = contract_split(prods, metric, dims) - contract_split(basis, middle, dims)
        second = contract_split(basis, metric, dims)
        high, low = split(jnp.concatenate([first + first, second + second], axis=1))
        where = pl.ds(i * piece, piece)
        split_ref[where, : 2 * width] = high
        split_ref[where, 2 * width : 4 * width] = low
        split_ref[where, 4 * width :] = high

    def body(step, carry):
        @pl.when(step + buffers - 1 < steps)
        def _():
            for copy in in_copies(step + buffers - 1):
                copy.start()

        for copy in in_copies(step):
            copy.wait()

        @pl.when(step >= buffers)
        def _():
            for copy in out_copies(step - buffers):
                copy.wait()

        slot = lax.rem(step, buffers)
        high, low = split(jnp.concatenate([la_ref[slot], lb_ref[slot]], axis=1))
        left = jnp.concatenate([high, high, low], axis=1)
        change = contract(left, split_ref[...], ((1,), (1,)))
        result_ref[slot] = in_ref[slot] - change
        for copy in out_copies(step):
            copy.start()
        return carry

    lax.fori_loop(0, steps, body, 0)
    for step in range(max(steps - buffers, 0), steps):
        for copy in out_copies(jnp.int32(step)):
            copy.wait()


def update(trailing, left_a, left_b, right_a, right_b, metric, middle, columns, order, start):
    height, depth = trailing.shape
    count = len(right_a)
    piece, width = right_a[0].shape
    _, block = blocking(height // order.shape[0], count)
    smem = pl.BlockSpec(memory_space=pltpu.SMEM)
    vmem = pl.BlockSpec(memory_space=pltpu.VMEM)
    hbm = pl.BlockSpec(memory_space=pl.ANY)
    args = [columns, order, trailing, left_a, left_b, *right_a, *right_b, metric, middle]
    in_specs = [smem, smem, hbm, hbm, hbm] + [vmem] * (2 * count + 2)
    aliases = {}
    if start is not None:
        aliases = {len(args): 0}
        args.append(start)
        in_specs.append(hbm)
    return pl.pallas_call(
        functools.partial(update_kernel, count, start is not None),
        in_specs=in_specs,
        out_specs=hbm,
        out_shape=jax.ShapeDtypeStruct((height, depth), F32),
        input_output_aliases=aliases,
        scratch_shapes=[
            pltpu.VMEM((count * piece, 6 * width), BF16),
            pltpu.VMEM((BUFFERS, block, count * piece), F32),
            pltpu.VMEM((BUFFERS, block, width), F32),
            pltpu.VMEM((BUFFERS, block, width), F32),
            pltpu.VMEM((BUFFERS, block, count * piece), F32),
            pltpu.SemaphoreType.DMA((BUFFERS, count + 2)),
            pltpu.SemaphoreType.DMA((BUFFERS, count)),
        ],
        compiler_params=pltpu.CompilerParams(vmem_limit_bytes=VMEM_LIMIT),
        name="update",
    )(*args)


def bits_of(size):
    return size.bit_length() - 1


def swap(block, axis, mask):
    size = lax.axis_size(axis)
    return lax.ppermute(block, axis, [(i, i ^ mask) for i in range(size)])


def sum_over_all(block):
    for axis in ("row", "col"):
        for bit in range(bits_of(lax.axis_size(axis))):
            other = swap(block, axis, 1 << bit)
            block = block + other
    return block


def stage_masks(count, stage):
    if stage == count - 1:
        return 1, 1
    return 1 << (stage + 1), 1 << (count - 1 - stage)


def stage_swap(block, axis, stage):
    size = lax.axis_size(axis)
    masks = stage_masks(bits_of(size), stage)
    return lax.ppermute(block, axis, [(i, i ^ masks[i & 1]) for i in range(size)])


def gather_masks(count, odd, stages):
    if stages == 0:
        return [0]
    mask = stage_masks(count, stages - 1)[odd]
    own = gather_masks(count, odd, stages - 1)
    other = gather_masks(count, odd ^ (mask & 1), stages - 1)
    return own + [mask ^ m for m in other]


def gather_over(block, axis):
    for stage in range(bits_of(lax.axis_size(axis))):
        other = stage_swap(block, axis, stage)
        block = jnp.concatenate([block, other])
    return block


def scatter_sum_over(block, axis):
    for stage in reversed(range(bits_of(lax.axis_size(axis)))):
        half = block.shape[0] // 2
        other = stage_swap(block[half:], axis, stage)
        block = block[:half] + other
    return block


def by_parity(index, even, odd):
    return jnp.where(index & 1 == 0, jnp.array(even, jnp.int32), jnp.array(odd, jnp.int32))


def rotate_right(index, size):
    return (index >> 1) | ((index & 1) * (size >> 1))


def rotate_left(index, size):
    return ((index << 1) & (size - 1)) | (index >> (bits_of(size) - 1))


def column_pieces(block):
    row_devices = lax.axis_size("row")
    col_devices = lax.axis_size("col")
    per_owner = col_devices // row_devices
    received = []
    for turn in range(row_devices):
        perm = []
        for r in range(row_devices):
            for c in range(col_devices):
                target_row = r ^ rotate_right(c % row_devices, row_devices) ^ turn
                target_col = per_owner * r + c // row_devices
                perm.append((r * col_devices + c, target_row * col_devices + target_col))
        received.append(lax.ppermute(block, ("row", "col"), perm))
    return received


def in_index_order(received, mask):
    count = bits_of(len(received))
    shape = received[0].shape
    pieces = jnp.stack(received).reshape((2,) * count + shape)
    for bit in range(count):
        pieces = jnp.where((mask >> bit) & 1 == 0, pieces, jnp.flip(pieces, count - 1 - bit))
    pieces = pieces.reshape((len(received),) + shape)
    order = [rotate_right(i, len(received)) for i in range(len(received))]
    return [jnp.concatenate([pieces[i] for i in order])]


def groups_of(groups, count):
    if count == sum(len(group) for group in groups):
        return groups
    return (tuple(range(count)),)


def on_device(trailing, panel_block):
    row_devices = lax.axis_size("row")
    col_devices = lax.axis_size("col")
    row = lax.axis_index("row")
    column = lax.axis_index("col")
    rows, width = panel_block.shape
    mask = row ^ (column // (col_devices // row_devices))
    count = bits_of(col_devices)
    order = column ^ by_parity(column, *[gather_masks(count, odd, count) for odd in (0, 1)])
    narrow = rows % 128 != 0

    gram_one = sum_over_all(matmul(panel_block.T, panel_block))
    upper_one, inverse_one = factor(gram_one)
    panel_rows = gather_over(panel_block, "col")
    panel_cols = column_pieces(panel_block)
    if narrow:
        panel_cols = in_index_order(panel_cols, mask)
    pieces = len(panel_cols)
    columns = [jnp.zeros((1,), jnp.int32) if narrow else rotate_left(mask ^ i, pieces)[None] for i in range(pieces)]

    def pick(group, blocks):
        return [blocks[i] for i in group], jnp.concatenate([columns[i] for i in group])

    first_cols = []
    for group in groups_of(PRODUCT_GROUPS, pieces):
        first_cols += basis_pieces([panel_cols[i] for i in group], inverse_one)
    own = matmul(panel_block, inverse_one.T)
    gram_two = matmul(own.T, own)
    partial = None
    for group in groups_of(PRODUCT_GROUPS, pieces):
        blocks, cols = pick(group, first_cols)
        partial = product(trailing, blocks, cols, order, partial)
    first_rows = matmul(panel_rows, inverse_one.T)
    inner = jnp.dot(first_rows.T, partial, preferred_element_type=F32, precision=lax.Precision.HIGH)
    sums = sum_over_all(jnp.concatenate([inner, gram_two]))
    inner, gram_two = sums[:width], sums[width:]
    mine = scatter_sum_over(partial, "col")
    product_cols = column_pieces(mine)
    if narrow:
        product_cols = in_index_order(product_cols, mask)
    product_rows = gather_over(mine, "col")

    upper_two, inverse_two = factor(gram_two)
    r_factor = matmul(upper_two, upper_one)
    metric = matmul(inverse_two.T, inverse_two)
    middle = matmul(matmul(metric, inner), metric)
    middle = middle + middle.T
    trailing_out = None
    for group in groups_of(UPDATE_GROUPS, pieces):
        right_a, cols = pick(group, first_cols)
        right_b, cols = pick(group, product_cols)
        trailing_out = update(
            trailing, first_rows, product_rows, right_a, right_b, metric, middle, cols, order, trailing_out
        )
    return (trailing_out, r_factor, upper_one)


def solution(mesh):
    in_specs = (P("row", "col"), P(("row", "col"), None))
    out_specs = (P("row", "col"), P(), P())

    return jax.shard_map(
        on_device, mesh=mesh, in_specs=in_specs, out_specs=out_specs, check_vma=False
    )
```
